32 devices in a mesh: strip: 4 (over y, core), depth: 8 (over z, x).
Axes of the slice: x: 2, y: 2, z: 4, core: 2. Of those that a mesh axis runs over, the one named last changes fastest.
Arguments:
- position: float32 [4, 8, 3, 32, 128], P('strip', 'depth'), may hold values from -2.4 to 2.4
- velocity: float32 [4, 8, 3, 32, 128], P('strip', 'depth'), may hold values from -3 to 3
- stress: float32 [4, 8, 6, 32, 128], P('strip', 'depth'), may hold values from -6 to 6
- plastic: float32 [4, 8, 32, 128], P('strip', 'depth'), may hold values from 0.005 to 0.2
- particle_mass: float32 [4, 8, 32, 128], P('strip', 'depth'), may hold values from 0.004 to 0.016
- density: float32 [4, 8, 32, 128], P('strip', 'depth'), may hold values from 0.6 to 1.6
- cohesion: float32 [4, 8, 32, 128], P('strip', 'depth'), may hold values from 0.3 to 1.2
- counts: int32 [4, 8, 32], P('strip', 'depth'), may hold values from 32 to 128, as said below
- block_pairs: int32 [4, 8, 128, 2], P('strip', 'depth'), may hold values from 0 to 31, as said below
- pair_count: int32 [4, 8], P('strip', 'depth'), may hold values from 32 to 128, as said below
- send_lists: int32 [4, 8, 4, 16], P('strip', 'depth'), may hold values from 0 to 31, as said below
- cross_links: int32 [4, 8, 2, 48, 2], P('strip', 'depth'), may hold values from 0 to 15, as said below
- contact: int32 [4, 8, 16], P('strip', 'depth'), may hold values from 0 to 32, as said below
Outputs:
- new_position: float32 [4, 8, 3, 32, 128], P('strip', 'depth')
- new_velocity: float32 [4, 8, 3, 32, 128], P('strip', 'depth')
- new_stress: float32 [4, 8, 6, 32, 128], P('strip', 'depth')
- new_plastic: float32 [4, 8, 32, 128], P('strip', 'depth')
The draws below stay inside these ranges and needn't reach their ends.
Inputs may be any that keep to these rules, and one draw needn't show every extreme that they name: A block's live particles are its first counts slots; every device has a full block. `pair_count`: at least 32; some device reaches 128. `block_pairs`: the first pair_count entries of a device hold each of its blocks paired with itself once and distinct unordered pairs of different blocks, each at most once, in either order; later entries are to be ignored. `send_lists`: each face lists 16 distinct blocks; faces 0, 1 look to the next and previous device along depth, 2, 3 along strip. `cross_links`: entry (f, q) = (a, b): slot a of the device's list 2f meets slot b of the next device's list 2f + 1; a face's entries are distinct. `contact`: 32 stands for no block; a device's entries are either all 32 or 16 distinct blocks.
All inputs are finite; a program needn't handle non-finite values.
Results may differ from the reference program's by a relative error of at most 0.0003.
Values sent between devices are 32-bit elements; how exact they have to be, the bound alone decides.
A program may use at most 64 MiB of HBM per device.

```python
import math
import jax
import jax.numpy as jnp
import numpy as np
from jax import lax

BLOCKS = 32
PARTICLES = 128
PAIR_RATIO = 3
RIM = 16
CROSS = 48
CONTACT = 16
RETURN_ITERS = 4
N_STRIP = 4
N_DEPTH = 8


def band_distance(key):
    centre = jax.random.randint(jax.random.fold_in(key, 101), (N_STRIP, 1), 0, N_DEPTH)
    depth_index = jnp.arange(N_DEPTH, dtype=jnp.int32)[None, :]
    return jnp.abs(depth_index - centre)


def pair_totals(key):
    distance = band_distance(key)
    band_width = max(N_DEPTH // 8, 1)
    off_most = PAIR_RATIO * BLOCKS
    jitter = jax.random.randint(jax.random.fold_in(key, 102), (N_STRIP, N_DEPTH), 0, off_most // 16 + 1)
    jitter = jnp.where(distance > 0, jitter, 0)
    off_live = off_most - jnp.minimum(distance, band_width) * (2 * off_most // 3) // band_width - jitter
    return (BLOCKS + off_live).astype(jnp.int32)


def draw_pair_count(key, part):
    return pair_totals(key)


def draw_block_pairs(key, part):
    totals = pair_totals(key).reshape(-1)
    upper_np, lower_np = np.triu_indices(BLOCKS, 1)
    upper_rows = jnp.asarray(upper_np, jnp.int32)
    upper_cols = jnp.asarray(lower_np, jnp.int32)
    off_most = PAIR_RATIO * BLOCKS
    slot_total = BLOCKS + off_most
    device_keys = jax.random.split(jax.random.fold_in(key, 103), N_STRIP * N_DEPTH)

    def one_device(device_key, live_total):
        pick_key, order_key, swap_key = jax.random.split(device_key, 3)
        chosen = jax.random.permutation(pick_key, upper_np.shape[0])[:off_most]
        diagonal_blocks = jnp.arange(BLOCKS, dtype=jnp.int32)
        row_block = jnp.concatenate([diagonal_blocks, upper_rows[chosen]])
        col_block = jnp.concatenate([diagonal_blocks, upper_cols[chosen]])
        reversed_pair = jax.random.randint(swap_key, (slot_total,), 0, 2)
        row_final = jnp.where(reversed_pair == 1, col_block, row_block)
        col_final = jnp.where(reversed_pair == 1, row_block, col_block)
        slot_index = jnp.arange(slot_total, dtype=jnp.int32)
        ranking = jax.random.permutation(order_key, slot_total).astype(jnp.int32)
        priority = jnp.where(slot_index < live_total, ranking, slot_total + slot_index)
        ordering = jnp.argsort(priority)
        return jnp.stack([row_final[ordering], col_final[ordering]], axis=-1).astype(jnp.int32)
    return jax.vmap(one_device)(device_keys, totals).reshape(N_STRIP, N_DEPTH, slot_total, 2)


def draw_send_lists(key, part):
    face_keys = jax.random.split(jax.random.fold_in(key, 104), N_STRIP * N_DEPTH * 4)

    def one_face(face_key):
        return jax.random.permutation(face_key, BLOCKS)[:RIM].astype(jnp.int32)
    return jax.vmap(one_face)(face_keys).reshape(N_STRIP, N_DEPTH, 4, RIM)


def draw_cross_links(key, part):
    face_keys = jax.random.split(jax.random.fold_in(key, 105), N_STRIP * N_DEPTH * 2)

    def one_face(face_key):
        picked = jax.random.permutation(face_key, RIM * RIM)[:CROSS].astype(jnp.int32)
        return jnp.stack([picked // RIM, picked % RIM], axis=-1)
    return jax.vmap(one_face)(face_keys).reshape(N_STRIP, N_DEPTH, 2, CROSS, 2)


def draw_contact(key, part):
    distance = band_distance(key).reshape(-1)
    device_keys = jax.random.split(jax.random.fold_in(key, 107), N_STRIP * N_DEPTH)

    def one_device(device_key, distance_one):
        picked = jax.random.permutation(device_key, BLOCKS)[:CONTACT].astype(jnp.int32)
        return jnp.where(distance_one <= 1, picked, BLOCKS).astype(jnp.int32)
    return jax.vmap(one_device)(device_keys, distance).reshape(N_STRIP, N_DEPTH, CONTACT)


def draw_counts(key, part):
    fill_key, full_key = jax.random.split(jax.random.fold_in(key, 106))
    counts = jax.random.randint(fill_key, (N_STRIP, N_DEPTH, BLOCKS), 32, PARTICLES + 1)
    full_block = jax.random.randint(full_key, (N_STRIP, N_DEPTH, 1), 0, BLOCKS)
    block_index = jnp.arange(BLOCKS, dtype=jnp.int32)[None, None, :]
    return jnp.where(block_index == full_block, PARTICLES, counts).astype(jnp.int32)


def level_of(key, extent, cuts, low, largest):
    def one(dim, shards_of):
        steps = jax.random.uniform(jax.random.fold_in(jax.random.fold_in(key, 6), dim), (shards_of,), jnp.float32, low / len(cuts), largest / len(cuts))
        return jnp.repeat(jnp.exp(steps), extent[dim] // shards_of).reshape((-1,) + (1,) * (len(extent) - dim - 1))

    loudness = one(*cuts[0])
    for cut in cuts[1:]:
        loudness = loudness * one(*cut)
    return loudness


def bell_draw(key, extent, scale, limit, cuts=(), kind=jnp.bfloat16):
    loudness = level_of(key, extent, cuts, -0.22, 0.18) if cuts else 1.0
    values = jax.random.normal(key, extent, jnp.float32) * scale * loudness
    return jnp.minimum(jnp.maximum(values, -limit), limit).astype(kind)


def setup_inputs(seed: int = 0) -> dict:
    key_of = jax.random.split(jax.random.key(seed), 14)
    position = bell_draw(key_of[0], (N_STRIP, N_DEPTH, 3, BLOCKS, PARTICLES), 0.4, 2.4, ((0, 4), (1, 8)), jnp.float32)
    velocity = bell_draw(key_of[1], (N_STRIP, N_DEPTH, 3, BLOCKS, PARTICLES), 0.5, 3.0, ((0, 4), (1, 8)), jnp.float32)
    stress = bell_draw(key_of[2], (N_STRIP, N_DEPTH, 6, BLOCKS, PARTICLES), 1.0, 6.0, ((0, 4), (1, 8)), jnp.float32)
    plastic = jnp.clip(jnp.exp(math.log(0.2) - 3.6888795 * jax.random.uniform(key_of[3], (N_STRIP, N_DEPTH, BLOCKS, PARTICLES), jnp.float32) ** level_of(key_of[3], (N_STRIP, N_DEPTH, BLOCKS, PARTICLES), ((0, 4), (1, 8)), -0.2, 0.2)), 0.005, 0.2)
    particle_mass = jnp.clip(jnp.exp(math.log(0.016) - 1.3862944 * jax.random.uniform(key_of[4], (N_STRIP, N_DEPTH, BLOCKS, PARTICLES), jnp.float32) ** level_of(key_of[4], (N_STRIP, N_DEPTH, BLOCKS, PARTICLES), ((0, 4), (1, 8)), -0.2, 0.2)), 0.004, 0.016)
    density = jnp.clip(jnp.exp(math.log(1.6) - 0.98082923 * jax.random.uniform(key_of[5], (N_STRIP, N_DEPTH, BLOCKS, PARTICLES), jnp.float32) ** level_of(key_of[5], (N_STRIP, N_DEPTH, BLOCKS, PARTICLES), ((0, 4), (1, 8)), -0.2, 0.2)), 0.6, 1.6)
    cohesion = jnp.clip(jnp.exp(math.log(1.2) - 1.3862944 * jax.random.uniform(key_of[6], (N_STRIP, N_DEPTH, BLOCKS, PARTICLES), jnp.float32) ** level_of(key_of[6], (N_STRIP, N_DEPTH, BLOCKS, PARTICLES), ((0, 4), (1, 8)), -0.2, 0.2)), 0.3, 1.2)
    counts = draw_counts(jax.random.fold_in(key_of[13], 71), 0)
    block_pairs = draw_block_pairs(jax.random.fold_in(key_of[13], 71), 0)
    pair_count = draw_pair_count(jax.random.fold_in(key_of[13], 71), 0)
    send_lists = draw_send_lists(jax.random.fold_in(key_of[13], 71), 0)
    cross_links = draw_cross_links(jax.random.fold_in(key_of[13], 71), 0)
    contact = draw_contact(jax.random.fold_in(key_of[13], 71), 0)
    return dict(position=position, velocity=velocity, stress=stress, plastic=plastic, particle_mass=particle_mass, density=density, cohesion=cohesion, counts=counts, block_pairs=block_pairs, pair_count=pair_count, send_lists=send_lists, cross_links=cross_links, contact=contact)


smooth_len = 1.5
kernel_coef = -105.0 / (3.141592653589793 * 1.5 ** 5)
time_step = 0.25
gravity = 1.0
spin_rate = 2.0
blade_stiff = 4.0
bulk_mod = 2.0
shear_mod = 1.5
friction = 0.25
harden_scale = 0.05
harden_mod = 0.5
relax_rate = 0.7
tau_floor = 0.5
voigt_index = ((0, 3, 5), (3, 1, 4), (5, 4, 2))
voigt_pairs = ((0, 0), (1, 1), (2, 2), (0, 1), (1, 2), (0, 2))

def source_rows(places, motion, stress, particle_mass, density, occupied):
    safe_density = jnp.where(occupied > 0.0, density, 1.0)
    weighted_mass = particle_mass * occupied
    volume = weighted_mass / safe_density
    scaled = stress / (safe_density * safe_density)[..., None, :]
    feature_rows = [weighted_mass]
    for row_axis in range(3):
        feature_rows.append(weighted_mass * places[..., row_axis, :])
    for component in range(6):
        feature_rows.append(weighted_mass * scaled[..., component, :])
    for row_axis in range(3):
        dotted = scaled[..., voigt_index[row_axis][0], :] * places[..., 0, :]
        dotted = dotted + scaled[..., voigt_index[row_axis][1], :] * places[..., 1, :]
        dotted = dotted + scaled[..., voigt_index[row_axis][2], :] * places[..., 2, :]
        feature_rows.append(weighted_mass * dotted)
    feature_rows.append(volume)
    for row_axis in range(3):
        feature_rows.append(volume * motion[..., row_axis, :])
    for row_axis in range(3):
        feature_rows.append(volume * places[..., row_axis, :])
    for row_axis, col_axis in voigt_pairs:
        paired = motion[..., row_axis, :] * places[..., col_axis, :] + motion[..., col_axis, :] * places[..., row_axis, :]
        feature_rows.append(volume * (0.5 * paired))
    return jnp.stack(feature_rows, axis=-2)

def pair_kernel(row_places, col_places, weight):
    squared = jnp.zeros(row_places.shape[:-2] + (row_places.shape[-1], col_places.shape[-1]), jnp.float32)
    for row_axis in range(3):
        spread = row_places[..., row_axis, :, None] - col_places[..., row_axis, None, :]
        squared = squared + spread * spread
    closeness = jnp.maximum(1.0 - jnp.sqrt(squared) / smooth_len, 0.0)
    return kernel_coef * closeness * closeness * closeness * weight[..., None, None]

def tile_terms(row_sources, row_places, col_sources, col_places, weight):
    kernel = pair_kernel(row_places, col_places, weight)
    to_rows = jnp.einsum('tkj,tij->tki', col_sources, kernel, precision=lax.Precision.HIGHEST)
    to_cols = jnp.einsum('tki,tij->tkj', row_sources, kernel, precision=lax.Precision.HIGHEST)
    return (to_rows, to_cols)

def section_rates(summed, places, motion, stress, density, contact_flag):
    scaled = stress / (density * density)[..., None, :]
    blade_motion = (spin_rate * places[..., 2, :], jnp.zeros_like(places[..., 1, :]), -spin_rate * places[..., 0, :])
    acceleration = []
    for row_axis in range(3):
        total_force = jnp.zeros_like(summed[..., 0, :])
        for col_axis in range(3):
            voigt_slot = voigt_index[row_axis][col_axis]
            total_force = total_force + scaled[..., voigt_slot, :] * (places[..., col_axis, :] * summed[..., 0, :] - summed[..., 1 + col_axis, :])
            total_force = total_force + places[..., col_axis, :] * summed[..., 4 + voigt_slot, :]
        total_force = total_force - summed[..., 10 + row_axis, :]
        total_force = total_force + blade_stiff * contact_flag * (blade_motion[row_axis] - motion[..., row_axis, :])
        if row_axis == 2:
            total_force = total_force - gravity
        acceleration.append(total_force)
    strain = []
    for component, (row_axis, col_axis) in enumerate(voigt_pairs):
        strain_rate = 0.5 * (places[..., col_axis, :] * summed[..., 14 + row_axis, :] + places[..., row_axis, :] * summed[..., 14 + col_axis, :])
        strain_rate = strain_rate - summed[..., 20 + component, :]
        strain_rate = strain_rate - 0.5 * summed[..., 13, :] * (motion[..., row_axis, :] * places[..., col_axis, :] + motion[..., col_axis, :] * places[..., row_axis, :])
        strain_rate = strain_rate + 0.5 * (motion[..., row_axis, :] * summed[..., 17 + col_axis, :] + motion[..., col_axis, :] * summed[..., 17 + row_axis, :])
        strain.append(strain_rate)
    return (jnp.stack(acceleration, axis=-2), jnp.stack(strain, axis=-2))

def elastic_step(stress, strain, fraction):
    volumetric = strain[..., 0, :] + strain[..., 1, :] + strain[..., 2, :]
    lame_first = bulk_mod - 2.0 * shear_mod / 3.0
    components = []
    for component in range(6):
        change = 2.0 * shear_mod * strain[..., component, :]
        if component < 3:
            change = change + lame_first * volumetric
        components.append(stress[..., component, :] + fraction * time_step * change)
    return components

def plastic_return(components, plastic, cohesion):
    for iteration in range(RETURN_ITERS):
        mean_stress = (components[0] + components[1] + components[2]) / 3.0
        deviator = [components[0] - mean_stress, components[1] - mean_stress, components[2] - mean_stress, components[3], components[4], components[5]]
        second = 0.5 * (deviator[0] * deviator[0] + deviator[1] * deviator[1] + deviator[2] * deviator[2])
        second = second + deviator[3] * deviator[3] + deviator[4] * deviator[4] + deviator[5] * deviator[5]
        shear_norm = jnp.sqrt(second)
        yield_limit = cohesion * (1.0 + plastic / (plastic + harden_scale))
        excess = jnp.maximum(shear_norm + friction * 3.0 * mean_stress - yield_limit, 0.0)
        multiplier = relax_rate * excess / (shear_mod + 9.0 * bulk_mod * friction * friction + harden_mod)
        shrink = jnp.maximum(1.0 - shear_mod * multiplier / jnp.maximum(shear_norm, tau_floor), 0.0)
        mean_stress = mean_stress - 3.0 * bulk_mod * friction * multiplier
        components = [deviator[0] * shrink + mean_stress, deviator[1] * shrink + mean_stress, deviator[2] * shrink + mean_stress, deviator[3] * shrink, deviator[4] * shrink, deviator[5] * shrink]
        plastic = plastic + multiplier
    return (jnp.stack(components, axis=-2), plastic)

def device_sums(sources, places, block_pairs, pair_count, send_lists, cross_links, depth_sources, depth_places, strip_sources, strip_places):
    slot_index = jnp.arange(block_pairs.shape[0], dtype=jnp.int32)
    row_block = block_pairs[:, 0]
    col_block = block_pairs[:, 1]
    weight = jnp.where(slot_index < pair_count, jnp.where(row_block == col_block, 0.5, 1.0), 0.0).astype(jnp.float32)
    to_rows, to_cols = tile_terms(sources[row_block], places[row_block], sources[col_block], places[col_block], weight)
    summed = jnp.zeros(sources.shape, jnp.float32).at[row_block].add(to_rows).at[col_block].add(to_cols)
    returned = []
    for face_index, far_sources, far_places in ((0, depth_sources, depth_places), (1, strip_sources, strip_places)):
        own_blocks = send_lists[2 * face_index][cross_links[face_index, :, 0]]
        far_slots = cross_links[face_index, :, 1]
        unit_weight = jnp.ones(far_slots.shape, jnp.float32)
        to_rows, to_cols = tile_terms(sources[own_blocks], places[own_blocks], far_sources[far_slots], far_places[far_slots], unit_weight)
        summed = summed.at[own_blocks].add(to_rows)
        returned.append(jnp.zeros(far_sources.shape, jnp.float32).at[far_slots].add(to_cols))
    return (summed, returned[0], returned[1])

def take_rows(table_in, index_list):
    return table_in[index_list]

def add_rows(table_in, index_list, extra):
    return table_in.at[index_list].add(extra)

def flatten_devices(values_in):
    return values_in.reshape((N_STRIP * N_DEPTH,) + values_in.shape[2:])

def unflatten_devices(values_in):
    return values_in.reshape((N_STRIP, N_DEPTH) + values_in.shape[1:])

def reference(position, velocity, stress, plastic, particle_mass, density, cohesion, counts, block_pairs, pair_count, send_lists, cross_links, contact):
    places = jnp.swapaxes(position, 2, 3)
    motion = jnp.swapaxes(velocity, 2, 3)
    stress_blocks = jnp.swapaxes(stress, 2, 3)
    occupied = (jnp.arange(PARTICLES, dtype=jnp.int32)[None, None, None, :] < counts[..., None]).astype(jnp.float32)
    contact_flag = lax.optimization_barrier(jnp.sum((contact[..., :, None] == jnp.arange(BLOCKS, dtype=jnp.int32)).astype(jnp.float32), axis=-2))[..., None]
    take_rim = jax.vmap(jax.vmap(take_rows))
    add_rim = jax.vmap(jax.vmap(add_rows))
    depth_keep = (jnp.arange(N_DEPTH) < N_DEPTH - 1).astype(jnp.float32)[None, :, None, None, None]
    depth_first = (jnp.arange(N_DEPTH) > 0).astype(jnp.float32)[None, :, None, None, None]

    def interact(cur_places, cur_motion, cur_stress):
        sources = source_rows(cur_places, cur_motion, cur_stress, particle_mass, density, occupied)
        depth_sources = jnp.roll(take_rim(sources, send_lists[:, :, 1]), -1, axis=1) * depth_keep
        depth_places = jnp.roll(take_rim(cur_places, send_lists[:, :, 1]), -1, axis=1) * depth_keep
        strip_sources = jnp.roll(take_rim(sources, send_lists[:, :, 3]), -1, axis=0)
        strip_places = jnp.roll(take_rim(cur_places, send_lists[:, :, 3]), -1, axis=0)

        def device_step(device_items):
            return device_sums(*device_items)
        gathered = tuple((flatten_devices(values_in) for values_in in (sources, cur_places, block_pairs, pair_count, send_lists, cross_links, depth_sources, depth_places, strip_sources, strip_places)))
        summed, back_depth, back_strip = lax.map(device_step, gathered)
        summed = unflatten_devices(summed)
        back_depth = jnp.roll(unflatten_devices(back_depth), 1, axis=1) * depth_first
        back_strip = jnp.roll(unflatten_devices(back_strip), 1, axis=0)
        summed = add_rim(summed, send_lists[:, :, 1], back_depth)
        summed = add_rim(summed, send_lists[:, :, 3], back_strip)
        return summed
    summed = interact(places, motion, stress_blocks)
    acceleration, strain = section_rates(summed, places, motion, stress_blocks, density, contact_flag)
    half_motion = motion + 0.5 * time_step * acceleration
    half_places = places + 0.5 * time_step * motion
    half_stress = plastic_return(elastic_step(stress_blocks, strain, 0.5), plastic, cohesion)[0]
    summed = interact(half_places, half_motion, half_stress)
    acceleration, strain = section_rates(summed, half_places, half_motion, half_stress, density, contact_flag)
    new_motion = motion + time_step * acceleration
    new_places = places + time_step * half_motion
    new_stress, new_plastic = plastic_return(elastic_step(stress_blocks, strain, 1.0), plastic, cohesion)
    particle_keep = occupied[..., None, :]
    return (jnp.swapaxes(new_places * particle_keep, 2, 3), jnp.swapaxes(new_motion * particle_keep, 2, 3), jnp.swapaxes(new_stress * particle_keep, 2, 3), new_plastic * occupied)
```

```python
import functools

import jax
import jax.numpy as jnp
from jax import lax
from jax.experimental import pallas as pl
from jax.experimental.pallas import tpu as pltpu
from jax.sharding import PartitionSpec as P

RETURN_ITERS = 4

smooth_len = 1.5
kernel_coef = -105.0 / (3.141592653589793 * 1.5**5)
time_step = 0.25
gravity = 1.0
spin_rate = 2.0
blade_stiff = 4.0
bulk_mod = 2.0
shear_mod = 1.5
friction = 0.25
harden_scale = 0.05
harden_mod = 0.5
relax_rate = 0.7
tau_floor = 0.5
voigt_index = ((0, 3, 5), (3, 1, 4), (5, 4, 2))
voigt_pairs = ((0, 0), (1, 1), (2, 2), (0, 1), (1, 2), (0, 2))

STATE = 16
SOURCES = 26
ROWS = 32
FEATURES = 32
UNROLL = 4
f32 = jnp.float32
bf16 = jnp.bfloat16


def from_behind(block, axis, distance):
    devices = range(lax.axis_size(axis))
    route = [(i - distance, i) for i in devices if i - distance in devices]
    return lax.ppermute(block, axis, route)


def passed_along(value, axis, steps):
    count = lax.axis_size(axis)
    pairs = [(source, (source + steps) % count) for source in range(count)]
    return lax.ppermute(value, axis, pairs)


def source_rows(x, v, s, mass, volume):
    rows = [mass]
    rows += [mass * x[k] for k in range(3)]
    rows += [mass * s[c] for c in range(6)]
    for k in range(3):
        i = voigt_index[k]
        rows.append(mass * (s[i[0]] * x[0] + s[i[1]] * x[1] + s[i[2]] * x[2]))
    rows.append(volume)
    rows += [volume * v[k] for k in range(3)]
    rows += [volume * x[k] for k in range(3)]
    for a, b in voigt_pairs:
        rows.append(volume * (0.5 * (v[a] * x[b] + v[b] * x[a])))
    return rows


def split3(value):
    high = value.astype(bf16).astype(f32)
    rest = value - high
    mid = rest.astype(bf16).astype(f32)
    low = (rest - mid).astype(bf16).astype(f32)
    return high, mid, low


PRODUCTS = ((0, 0), (0, 1), (1, 0), (1, 1), (0, 2), (2, 0))


def distance_rows(x, row_side, col_side):
    scaled = [x[k] * (1.0 / smooth_len) for k in range(3)]
    parts = [split3(y) for y in scaled]
    norm = split3(scaled[0] * scaled[0] + scaled[1] * scaled[1] + scaled[2] * scaled[2])
    one = jnp.ones_like(x[0])
    zero = jnp.zeros_like(x[0])
    left, right = [], []
    for k in range(3):
        for a, b in PRODUCTS:
            left.append(-2.0 * parts[k][a])
            right.append(parts[k][b])
    left += list(norm) + [one] * 3
    right += [one] * 3 + list(norm)
    fill = FEATURES - len(left)
    return (left + [zero] * fill if row_side else None, right + [zero] * fill if col_side else None)


def put_rows(ref, rows, start, count, stride):
    for k, row in enumerate(rows):
        ref[pl.ds(start * stride + k, count, stride=stride), :] = row


def get_row(ref, k, count, stride):
    return ref[pl.ds(k, count, stride=stride), :]


def close_kernel(left, right, weight):
    squared = lax.dot_general(left, right, (((1,), (0,)), ((), ())), preferred_element_type=f32)
    squared = jnp.maximum(squared, 1e-30)
    near = jnp.maximum(1.0 - squared * lax.rsqrt(squared), 0.0)
    cubed = near * near * (near if weight is None else near * weight)
    return cubed.astype(bf16)


def fold(result):
    return result[:ROWS] + result[ROWS:]


def to_rows(sources, kernel):
    return fold(
        lax.dot_general(sources, kernel, (((1,), (1,)), ((), ())), preferred_element_type=f32)
    )


def to_cols(sources, kernel):
    return fold(
        lax.dot_general(sources, kernel, (((1,), (0,)), ((), ())), preferred_element_type=f32)
    )


def store_sources(tmp, src, start, count):
    def one(b, carry):
        rows = tmp[pl.ds(pl.multiple_of(b * ROWS, ROWS), ROWS), :]
        high = rows.astype(bf16)
        src[start + b, 0:ROWS, :] = high
        src[start + b, ROWS : 2 * ROWS, :] = (rows - high.astype(f32)).astype(bf16)
        return carry

    lax.fori_loop(0, count, one, 0, unroll=4)


def store_cols(tmp, col, start, count):
    def one(b, carry):
        col[start + b] = tmp[pl.ds(pl.multiple_of(b * FEATURES, FEATURES), FEATURES), :].astype(bf16)
        return carry

    lax.fori_loop(0, count, one, 0, unroll=4)


def gather_rims(rows, raw, lists, sends, blocks):
    put_rows(raw, rows, 0, blocks, STATE)
    for face in range(4):
        for slot in range(lists.shape[1]):
            at = pl.multiple_of(lists[face, slot] * STATE, STATE)
            sends[face][slot * STATE : (slot + 1) * STATE, :] = raw[pl.ds(at, STATE), :]


def begin_kernel(
    counts, lists, pos, vel, stress, mass, density, state, s0, s1, s2, s3, occ, raw
):
    blocks, parts = mass.shape
    lane = lax.broadcasted_iota(jnp.int32, (1, parts), 1)
    for b in range(blocks):
        occ[b : b + 1, :] = jnp.where(lane < counts[b], 1.0, 0.0)
    live = occ[...]
    rho = density[...]
    inverse = 1.0 / (rho * rho)
    weighted = mass[...] * live * kernel_coef
    rows = [pos[k] for k in range(3)] + [vel[k] for k in range(3)]
    rows += [stress[c] * inverse for c in range(6)]
    rows += [weighted, weighted / rho, live, inverse]
    for k, row in enumerate(rows):
        state[k] = row
    gather_rims(rows, raw, lists, (s0, s1, s2, s3), blocks)


def local_kernel(pairs, total, state, acc, left, tmp, src, right):
    blocks = state.shape[1]
    x = [state[k] for k in range(3)]
    v = [state[k] for k in range(3, 6)]
    s = [state[k] for k in range(6, 12)]
    zero = jnp.zeros_like(x[0])
    rows = source_rows(x, v, s, state[12], state[13])
    put_rows(tmp, rows + [zero] * (ROWS - SOURCES), 0, blocks, ROWS)
    store_sources(tmp, src, 0, blocks)
    left_rows, right_rows = distance_rows(x, True, True)
    put_rows(tmp, right_rows, 0, blocks, FEATURES)
    store_cols(tmp, right, 0, blocks)
    put_rows(tmp, left_rows, 0, blocks, FEATURES)

    def turn(b, carry):
        block = tmp[pl.ds(pl.multiple_of(b * FEATURES, FEATURES), FEATURES), :]
        left[b] = block.T.astype(bf16)
        acc[b] = jnp.zeros(acc.shape[1:], f32)
        return carry

    lax.fori_loop(0, blocks, turn, 0, unroll=4)
    live = total[0, 0]
    last = pairs.shape[0] - 1

    def group(g, carry):
        found = []
        for u in range(UNROLL):
            q = g * UNROLL + u
            at = jnp.minimum(q, last)
            a, b = pairs[at, 0], pairs[at, 1]
            a = jnp.where(q < live, a, 0)
            b = jnp.where(q < live, b, 0)
            weight = jnp.where(q < live, jnp.where(a == b, 0.5, 1.0), 0.0)
            kernel = close_kernel(left[a], right[b], weight)
            found.append((a, to_rows(src[b], kernel)))
            found.append((b, to_cols(src[a], kernel)))
        for at, value in found:
            acc[at] += value
        return carry

    lax.fori_loop(0, (live + UNROLL - 1) // UNROLL, group, 0)


def cross_sums(lists, links, links_behind, far, acc_in, left, acc, tmp, src, right):
    rim = lists.shape[1]
    for f in range(4):
        got = [get_row(far[f], k, rim, STATE) for k in range(14)]
        zero = jnp.zeros_like(got[0])
        rows = source_rows(got[0:3], got[3:6], got[6:12], got[12], got[13])
        put_rows(tmp, rows + [zero] * (ROWS - SOURCES), f * rim, rim, ROWS)
    store_sources(tmp, src, 0, 4 * rim)
    for f in range(4):
        got = [get_row(far[f], k, rim, STATE) for k in range(3)]
        put_rows(tmp, distance_rows(got, False, True)[1], f * rim, rim, FEATURES)
    store_cols(tmp, right, 0, 4 * rim)
    acc[...] = acc_in[...]

    def group(q, carry):
        found = []
        for face in range(2):
            own = lists[2 * face, links[face, q, 0]]
            slot = 2 * face * rim + links[face, q, 1]
            found.append((own, to_rows(src[slot], close_kernel(left[own], right[slot], None))))
            own = lists[2 * face + 1, links_behind[face][q, 1]]
            slot = (2 * face + 1) * rim + links_behind[face][q, 0]
            found.append((own, to_rows(src[slot], close_kernel(left[own], right[slot], None))))
        for at, value in found:
            acc[at] += value
        return carry

    lax.fori_loop(0, links.shape[1], group, 0)


def section_rates(summed, x, v, s, contact_flag):
    blade = (spin_rate * x[2], jnp.zeros_like(x[1]), -spin_rate * x[0])
    acceleration = []
    arm = [x[l] * summed[0] - summed[1 + l] for l in range(3)]
    for k in range(3):
        total = -summed[10 + k] + blade_stiff * contact_flag * (blade[k] - v[k])
        for l in range(3):
            slot = voigt_index[k][l]
            total = total + s[slot] * arm[l] + x[l] * summed[4 + slot]
        if k == 2:
            total = total - gravity
        acceleration.append(total)
    strain = []
    for c, (k, l) in enumerate(voigt_pairs):
        rate = 0.5 * (x[l] * summed[14 + k] + x[k] * summed[14 + l]) - summed[20 + c]
        rate = rate - 0.5 * summed[13] * (v[k] * x[l] + v[l] * x[k])
        rate = rate + 0.5 * (v[k] * summed[17 + l] + v[l] * summed[17 + k])
        strain.append(rate)
    return acceleration, strain


def elastic_step(stress, strain, fraction):
    volumetric = strain[0] + strain[1] + strain[2]
    lame_first = bulk_mod - 2.0 * shear_mod / 3.0
    components = []
    for c in range(6):
        change = 2.0 * shear_mod * strain[c]
        if c < 3:
            change = change + lame_first * volumetric
        components.append(stress[c] + fraction * time_step * change)
    return components


def plastic_return(c, plastic, cohesion):
    for _ in range(RETURN_ITERS):
        mean = (c[0] + c[1] + c[2]) / 3.0
        d = [c[0] - mean, c[1] - mean, c[2] - mean, c[3], c[4], c[5]]
        second = 0.5 * (d[0] * d[0] + d[1] * d[1] + d[2] * d[2])
        second = second + d[3] * d[3] + d[4] * d[4] + d[5] * d[5]
        tau = jnp.sqrt(second)
        limit = cohesion * (1.0 + plastic / (plastic + harden_scale))
        excess = jnp.maximum(tau + friction * 3.0 * mean - limit, 0.0)
        multiplier = (
            relax_rate * excess / (shear_mod + 9.0 * bulk_mod * friction * friction + harden_mod)
        )
        shrink = jnp.maximum(1.0 - shear_mod * multiplier / jnp.maximum(tau, tau_floor), 0.0)
        mean = mean - 3.0 * bulk_mod * friction * multiplier
        c = [
            d[0] * shrink + mean,
            d[1] * shrink + mean,
            d[2] * shrink + mean,
            d[3] * shrink,
            d[4] * shrink,
            d[5] * shrink,
        ]
        plastic = plastic + multiplier
    return c, plastic


def contact_rows(contact, flag, blocks):
    flag[...] = jnp.zeros_like(flag)
    for i in range(contact.shape[0]):
        flag[pl.ds(contact[i], 1), :] += 1.0
    return flag[0:blocks, :]


def rates_of(acc, state, contact, flag):
    blocks, parts = state.shape[1:]
    contact_flag = contact_rows(contact, flag, blocks)
    x = [state[k] for k in range(3)]
    v = [state[k] for k in range(3, 6)]
    s = [state[k] for k in range(6, 12)]
    summed = [acc[:, k, :] for k in range(SOURCES)]
    return x, v, *section_rates(summed, x, v, s, contact_flag)


def half_kernel(
    lists, links, behind_depth, behind_strip, contact,
    acc_in, left, d_next, d_prev, s_next, s_prev, state, stress, plastic, cohesion,
    state_out, s0, s1, s2, s3,
    acc, tmp, src, right, flag, raw,
):
    blocks = state.shape[1]
    cross_sums(
        lists, links, (behind_depth, behind_strip), (d_next, d_prev, s_next, s_prev),
        acc_in, left, acc, tmp, src, right,
    )
    x, v, acceleration, strain = rates_of(acc, state, contact, flag)
    components, _ = plastic_return(
        elastic_step([stress[c] for c in range(6)], strain, 0.5), plastic[...], cohesion[...]
    )
    inverse = state[15]
    rows = [x[k] + 0.5 * time_step * v[k] for k in range(3)]
    rows += [v[k] + 0.5 * time_step * acceleration[k] for k in range(3)]
    rows += [c * inverse for c in components]
    rows += [state[12], state[13], state[14], inverse]
    for k, row in enumerate(rows):
        state_out[k] = row
    gather_rims(rows, raw, lists, (s0, s1, s2, s3), blocks)


def end_kernel(
    lists, links, behind_depth, behind_strip, contact,
    acc_in, left, d_next, d_prev, s_next, s_prev, state, stress, plastic, cohesion, position, velocity,
    new_position, new_velocity, new_stress, new_plastic,
    acc, tmp, src, right, flag,
):
    cross_sums(
        lists, links, (behind_depth, behind_strip), (d_next, d_prev, s_next, s_prev),
        acc_in, left, acc, tmp, src, right,
    )
    _, half_v, acceleration, strain = rates_of(acc, state, contact, flag)
    components, hardened = plastic_return(
        elastic_step([stress[c] for c in range(6)], strain, 1.0), plastic[...], cohesion[...]
    )
    live = state[14]
    for k in range(3):
        new_position[k] = (position[k] + time_step * half_v[k]) * live
        new_velocity[k] = (velocity[k] + time_step * acceleration[k]) * live
    for c in range(6):
        new_stress[c] = components[c] * live
    new_plastic[...] = hardened * live


def shards(
    position, velocity, stress, plastic, particle_mass, density, cohesion,
    counts, block_pairs, pair_count, send_lists, cross_links, contact,
):
    position, velocity, stress = position[0, 0], velocity[0, 0], stress[0, 0]
    plastic, mass, density, cohesion = plastic[0, 0], particle_mass[0, 0], density[0, 0], cohesion[0, 0]
    counts, pairs, lists = counts[0, 0], block_pairs[0, 0], send_lists[0, 0]
    links, contact = cross_links[0, 0], contact[0, 0]
    blocks, parts = mass.shape
    rim = lists.shape[1]
    smem = pl.BlockSpec(memory_space=pltpu.SMEM)
    vmem = pl.BlockSpec(memory_space=pltpu.VMEM)
    shape = jax.ShapeDtypeStruct
    state_shape = shape((STATE, blocks, parts), f32)
    send_shape = shape((rim * STATE, parts), f32)
    acc_shape = shape((blocks, ROWS, parts), f32)
    left_shape = shape((blocks, parts, FEATURES), bf16)
    far_scratch = [
        pltpu.VMEM((blocks, ROWS, parts), f32),
        pltpu.VMEM((4 * rim * ROWS, parts), f32),
        pltpu.VMEM((4 * rim, 2 * ROWS, parts), bf16),
        pltpu.VMEM((4 * rim, FEATURES, parts), bf16),
        pltpu.VMEM((blocks + 8, parts), f32),
    ]
    raw_scratch = pltpu.VMEM((blocks * STATE, parts), f32)
    params = pltpu.CompilerParams(vmem_limit_bytes=24 << 20)

    behind_depth = from_behind(links[0], "depth", 1)
    behind_strip = passed_along(links[1], "strip", 1)

    def exchange(sends):
        return (
            from_behind(sends[1], "depth", -1),
            from_behind(sends[0], "depth", 1),
            passed_along(sends[3], "strip", -1),
            passed_along(sends[2], "strip", 1),
        )

    def local(state):
        tiles = pairs.shape[0]
        return pl.pallas_call(
            local_kernel,
            out_shape=(acc_shape, left_shape),
            in_specs=[smem, smem, vmem],
            out_specs=(vmem, vmem),
            scratch_shapes=[
                pltpu.VMEM((blocks * ROWS, parts), f32),
                pltpu.VMEM((blocks, 2 * ROWS, parts), bf16),
                pltpu.VMEM((blocks, FEATURES, parts), bf16),
            ],
            compiler_params=params,
            cost_estimate=pl.CostEstimate(
                flops=tiles * parts * parts * 600, bytes_accessed=8 << 20, transcendentals=0
            ),
            name="local_tiles",
        )(pairs, pair_count, state)

    state, *sends = pl.pallas_call(
        begin_kernel,
        out_shape=(state_shape,) + (send_shape,) * 4,
        in_specs=[smem] * 2 + [vmem] * 5,
        out_specs=(vmem,) * 5,
        scratch_shapes=[pltpu.VMEM((blocks, parts), f32), raw_scratch],
        compiler_params=params,
        name="begin",
    )(counts, lists, position, velocity, stress, mass, density)
    far = exchange(sends)
    acc, left = local(state)
    half, *sends = pl.pallas_call(
        half_kernel,
        out_shape=(state_shape,) + (send_shape,) * 4,
        in_specs=[smem] * 5 + [vmem] * 10,
        out_specs=(vmem,) * 5,
        scratch_shapes=far_scratch + [raw_scratch],
        compiler_params=params,
        name="half_step",
    )(
        lists, links, behind_depth, behind_strip, contact,
        acc, left, *far, state, stress, plastic, cohesion,
    )
    far = exchange(sends)
    acc, left = local(half)
    outs = pl.pallas_call(
        end_kernel,
        out_shape=(
            shape(position.shape, f32),
            shape(velocity.shape, f32),
            shape(stress.shape, f32),
            shape(plastic.shape, f32),
        ),
        in_specs=[smem] * 5 + [vmem] * 12,
        out_specs=(vmem,) * 4,
        scratch_shapes=far_scratch,
        compiler_params=params,
        name="full_step",
    )(
        lists, links, behind_depth, behind_strip, contact,
        acc, left, *far, half, stress, plastic, cohesion, position, velocity,
    )
    return tuple(out[None, None] for out in outs)


def solution(mesh):
    def spec(rank):
        return P("strip", "depth", *([None] * (rank - 2)))

    return jax.shard_map(
        shards,
        mesh=mesh,
        in_specs=tuple(spec(r) for r in (5, 5, 5, 4, 4, 4, 4, 3, 4, 2, 4, 5, 3)),
        out_specs=tuple(spec(r) for r in (5, 5, 5, 4)),
        check_vma=False,
    )
```

```python
import functools

import jax
import jax.numpy as jnp
from jax import lax
from jax.experimental import pallas as pl
from jax.experimental.pallas import tpu as pltpu
from jax.sharding import PartitionSpec as P

RETURN_ITERS = 4

smooth_len = 1.5
kernel_coef = -105.0 / (3.141592653589793 * 1.5**5)
time_step = 0.25
gravity = 1.0
spin_rate = 2.0
blade_stiff = 4.0
bulk_mod = 2.0
shear_mod = 1.5
friction = 0.25
harden_scale = 0.05
harden_mod = 0.5
relax_rate = 0.7
tau_floor = 0.5
voigt_index = ((0, 3, 5), (3, 1, 4), (5, 4, 2))
voigt_pairs = ((0, 0), (1, 1), (2, 2), (0, 1), (1, 2), (0, 2))

STATE = 16
SOURCES = 26
ROWS = 32
FEATURES = 32
UNROLL = 4
PITCH = 36
f32 = jnp.float32
bf16 = jnp.bfloat16


def from_behind(block, axis, distance):
    devices = range(lax.axis_size(axis))
    route = [(i - distance, i) for i in devices if i - distance in devices]
    return lax.ppermute(block, axis, route)


def passed_along(value, axis, steps):
    count = lax.axis_size(axis)
    pairs = [(source, (source + steps) % count) for source in range(count)]
    return lax.ppermute(value, axis, pairs)


def source_rows(x, v, s, mass, volume):
    rows = [mass]
    rows += [mass * x[k] for k in range(3)]
    rows += [mass * s[c] for c in range(6)]
    for k in range(3):
        i = voigt_index[k]
        rows.append(mass * (s[i[0]] * x[0] + s[i[1]] * x[1] + s[i[2]] * x[2]))
    rows.append(volume)
    rows += [volume * v[k] for k in range(3)]
    rows += [volume * x[k] for k in range(3)]
    for a, b in voigt_pairs:
        rows.append(volume * (0.5 * (v[a] * x[b] + v[b] * x[a])))
    return rows


def split3(value):
    high = value.astype(bf16).astype(f32)
    rest = value - high
    mid = rest.astype(bf16).astype(f32)
    low = (rest - mid).astype(bf16).astype(f32)
    return high, mid, low


PRODUCTS = ((0, 0), (0, 1), (1, 0), (1, 1), (0, 2), (2, 0))


def distance_rows(x, row_side, col_side):
    scaled = [x[k] * (1.0 / smooth_len) for k in range(3)]
    parts = [split3(y) for y in scaled]
    norm = split3(scaled[0] * scaled[0] + scaled[1] * scaled[1] + scaled[2] * scaled[2])
    one = jnp.ones_like(x[0])
    zero = jnp.zeros_like(x[0])
    left, right = [], []
    for k in range(3):
        for a, b in PRODUCTS:
            left.append(-2.0 * parts[k][a])
            right.append(parts[k][b])
    left += list(norm) + [one] * 3
    right += [one] * 3 + list(norm)
    fill = FEATURES - len(left)
    return (left + [zero] * fill if row_side else None, right + [zero] * fill if col_side else None)


def put_rows(ref, rows, start, count, stride):
    for k, row in enumerate(rows):
        ref[pl.ds(start * stride + k, count, stride=stride), :] = row


def get_row(ref, k, count, stride):
    return ref[pl.ds(k, count, stride=stride), :]


def close_kernel(left, right, weight):
    squared = lax.dot_general(left, right, (((1,), (0,)), ((), ())), preferred_element_type=f32)
    squared = jnp.maximum(squared, 1e-30)
    near = jnp.maximum(1.0 - squared * lax.rsqrt(squared), 0.0)
    cubed = near * near * (near if weight is None else near * weight)
    return cubed.astype(bf16)


def fold(result):
    return result[:ROWS] + result[ROWS:]


def to_rows(sources, kernel):
    return fold(
        lax.dot_general(sources, kernel, (((1,), (1,)), ((), ())), preferred_element_type=f32)
    )


def to_cols(sources, kernel):
    return fold(
        lax.dot_general(sources, kernel, (((1,), (0,)), ((), ())), preferred_element_type=f32)
    )


def pipelined(groups, width, prepare, apply, acc):
    for u in range(width):
        prepare(0, u, 0)

    def step(i, carry):
        for half in range(2):
            g = 2 * i + half
            found = []
            for u in range(width):
                found += apply(g, u, half)
                prepare(g + 1, u, 1 - half)
            for at, value in found:
                acc[at] += value
        return carry

    lax.fori_loop(0, (groups + 1) // 2, step, 0)


def store_sources(tmp, src, start, count):
    def one(b, carry):
        rows = tmp[pl.ds(b * PITCH, ROWS), :]
        high = rows.astype(bf16)
        src[start + b, 0:ROWS, :] = high
        src[start + b, ROWS : 2 * ROWS, :] = (rows - high.astype(f32)).astype(bf16)
        return carry

    lax.fori_loop(0, count, one, 0, unroll=4)


def store_cols(tmp, col, start, count):
    def one(b, carry):
        col[start + b] = tmp[pl.ds(b * PITCH, FEATURES), :].astype(bf16)
        return carry

    lax.fori_loop(0, count, one, 0, unroll=4)


def store_lefts(tmp, left, start, count):
    def one(b, carry):
        left[start + b] = tmp[pl.ds(b * PITCH, FEATURES), :].T.astype(bf16)
        return carry

    lax.fori_loop(0, count, one, 0, unroll=4)


def gather_rims(rows, raw, lists, sends, blocks):
    put_rows(raw, rows, 0, blocks, STATE)
    for face in range(4):
        for slot in range(lists.shape[1]):
            at = pl.multiple_of(lists[face, slot] * STATE, STATE)
            sends[face][slot * STATE : (slot + 1) * STATE, :] = raw[pl.ds(at, STATE), :]


def begin_kernel(
    counts, lists, pos_in, vel_in, stress_in, mass_in, density_in, state, s0, s1, s2, s3,
    occ, raw, pos, vel, stress, mass, density, sems,
):
    moved = ((pos_in, pos), (vel_in, vel), (stress_in, stress), (mass_in, mass), (density_in, density))
    copies = [pltpu.make_async_copy(a, b, sems.at[i]) for i, (a, b) in enumerate(moved)]
    for copy in copies:
        copy.start()
    blocks, parts = mass.shape
    lane = lax.broadcasted_iota(jnp.int32, (1, parts), 1)
    for b in range(blocks):
        occ[b : b + 1, :] = jnp.where(lane < counts[b], 1.0, 0.0)
    live = occ[...]
    for copy in copies:
        copy.wait()
    rho = density[...]
    inverse = 1.0 / (rho * rho)
    weighted = mass[...] * live * kernel_coef
    rows = [pos[k] for k in range(3)] + [vel[k] for k in range(3)]
    rows += [stress[c] * inverse for c in range(6)]
    rows += [weighted, weighted / rho, live, inverse]
    for k, row in enumerate(rows):
        state[k] = row
    gather_rims(rows, raw, lists, (s0, s1, s2, s3), blocks)


def local_kernel(pairs, total, state, acc, right, tmp, src, left, held):
    blocks = state.shape[1]
    x = [state[k] for k in range(3)]
    v = [state[k] for k in range(3, 6)]
    s = [state[k] for k in range(6, 12)]
    zero = jnp.zeros_like(x[0])
    rows = source_rows(x, v, s, state[12], state[13])
    put_rows(tmp, rows + [zero] * (ROWS - SOURCES), 0, blocks, PITCH)
    store_sources(tmp, src, 0, blocks)
    left_rows, right_rows = distance_rows(x, True, True)
    put_rows(tmp, right_rows, 0, blocks, PITCH)
    store_cols(tmp, right, 0, blocks)
    put_rows(tmp, left_rows, 0, blocks, PITCH)

    store_lefts(tmp, left, 0, blocks)
    acc[...] = jnp.zeros(acc.shape, f32)
    live = total[0, 0]
    last = pairs.shape[0] - 1

    def entry(q):
        at = jnp.minimum(q, last)
        a, b = pairs[at, 0], pairs[at, 1]
        return jnp.where(q < live, a, 0), jnp.where(q < live, b, 0)

    def prepare(g, u, slot):
        q = g * UNROLL + u
        a, b = entry(q)
        weight = jnp.where(q < live, jnp.where(a == b, 0.5, 1.0), 0.0)
        held[slot * UNROLL + u] = close_kernel(left[a], right[b], weight)

    def apply(g, u, slot):
        a, b = entry(g * UNROLL + u)
        kernel = held[slot * UNROLL + u]
        return [(a, to_rows(src[b], kernel)), (b, to_cols(src[a], kernel))]

    pipelined((live + UNROLL - 1) // UNROLL, UNROLL, prepare, apply, acc)


def cross_sums(lists, links, links_behind, far, acc_in, right, acc, tmp, src, left, held):
    rim = lists.shape[1]
    for f in range(4):
        got = [get_row(far[f], k, rim, STATE) for k in range(14)]
        zero = jnp.zeros_like(got[0])
        rows = source_rows(got[0:3], got[3:6], got[6:12], got[12], got[13])
        put_rows(tmp, rows + [zero] * (ROWS - SOURCES), f * rim, rim, PITCH)
    store_sources(tmp, src, 0, 4 * rim)
    for f in range(4):
        got = [get_row(far[f], k, rim, STATE) for k in range(3)]
        put_rows(tmp, distance_rows(got, True, False)[0], f * rim, rim, PITCH)
    store_lefts(tmp, left, 0, 4 * rim)
    acc[...] = acc_in[...]

    last = links.shape[1] - 1

    def entry(q, u):
        at = jnp.minimum(q, last)
        face, behind = u // 2, u % 2
        if behind:
            own = lists[2 * face + 1, links_behind[face][at, 1]]
            return own, u * rim + links_behind[face][at, 0]
        return lists[2 * face, links[face, at, 0]], u * rim + links[face, at, 1]

    def prepare(q, u, slot):
        own, far_slot = entry(q, u)
        weight = None if links.shape[1] % 2 == 0 else jnp.where(q <= last, 1.0, 0.0)
        held[slot * 4 + u] = close_kernel(left[far_slot], right[own], weight)

    def apply(q, u, slot):
        own, far_slot = entry(q, u)
        return [(own, to_cols(src[far_slot], held[slot * 4 + u]))]

    pipelined(links.shape[1], 4, prepare, apply, acc)


def section_rates(summed, x, v, s, contact_flag):
    blade = (spin_rate * x[2], jnp.zeros_like(x[1]), -spin_rate * x[0])
    acceleration = []
    arm = [x[l] * summed[0] - summed[1 + l] for l in range(3)]
    for k in range(3):
        total = -summed[10 + k] + blade_stiff * contact_flag * (blade[k] - v[k])
        for l in range(3):
            slot = voigt_index[k][l]
            total = total + s[slot] * arm[l] + x[l] * summed[4 + slot]
        if k == 2:
            total = total - gravity
        acceleration.append(total)
    strain = []
    for c, (k, l) in enumerate(voigt_pairs):
        rate = 0.5 * (x[l] * summed[14 + k] + x[k] * summed[14 + l]) - summed[20 + c]
        rate = rate - 0.5 * summed[13] * (v[k] * x[l] + v[l] * x[k])
        rate = rate + 0.5 * (v[k] * summed[17 + l] + v[l] * summed[17 + k])
        strain.append(rate)
    return acceleration, strain


def elastic_step(stress, strain, fraction):
    volumetric = strain[0] + strain[1] + strain[2]
    lame_first = bulk_mod - 2.0 * shear_mod / 3.0
    components = []
    for c in range(6):
        change = 2.0 * shear_mod * strain[c]
        if c < 3:
            change = change + lame_first * volumetric
        components.append(stress[c] + fraction * time_step * change)
    return components


def plastic_return(c, plastic, cohesion):
    for _ in range(RETURN_ITERS):
        mean = (c[0] + c[1] + c[2]) / 3.0
        d = [c[0] - mean, c[1] - mean, c[2] - mean, c[3], c[4], c[5]]
        second = 0.5 * (d[0] * d[0] + d[1] * d[1] + d[2] * d[2])
        second = second + d[3] * d[3] + d[4] * d[4] + d[5] * d[5]
        tau = jnp.sqrt(second)
        limit = cohesion * (1.0 + plastic / (plastic + harden_scale))
        excess = jnp.maximum(tau + friction * 3.0 * mean - limit, 0.0)
        multiplier = (
            relax_rate * excess / (shear_mod + 9.0 * bulk_mod * friction * friction + harden_mod)
        )
        shrink = jnp.maximum(1.0 - shear_mod * multiplier / jnp.maximum(tau, tau_floor), 0.0)
        mean = mean - 3.0 * bulk_mod * friction * multiplier
        c = [
            d[0] * shrink + mean,
            d[1] * shrink + mean,
            d[2] * shrink + mean,
            d[3] * shrink,
            d[4] * shrink,
            d[5] * shrink,
        ]
        plastic = plastic + multiplier
    return c, plastic


def contact_rows(contact, flag, blocks):
    flag[...] = jnp.zeros_like(flag)
    for i in range(contact.shape[0]):
        flag[pl.ds(contact[i], 1), :] += 1.0
    return flag[0:blocks, :]


def rates_of(acc, state, contact, flag):
    blocks, parts = state.shape[1:]
    contact_flag = contact_rows(contact, flag, blocks)
    x = [state[k] for k in range(3)]
    v = [state[k] for k in range(3, 6)]
    s = [state[k] for k in range(6, 12)]
    summed = [acc[:, k, :] for k in range(SOURCES)]
    return x, v, *section_rates(summed, x, v, s, contact_flag)


def half_kernel(
    lists, links, behind_depth, behind_strip, contact,
    acc_in, right, d_next, d_prev, s_next, s_prev, state, stress, plastic, cohesion,
    state_out, s0, s1, s2, s3,
    acc, tmp, src, left, held, flag, raw,
):
    blocks = state.shape[1]
    cross_sums(
        lists, links, (behind_depth, behind_strip), (d_next, d_prev, s_next, s_prev),
        acc_in, right, acc, tmp, src, left, held,
    )
    x, v, acceleration, strain = rates_of(acc, state, contact, flag)
    components, _ = plastic_return(
        elastic_step([stress[c] for c in range(6)], strain, 0.5), plastic[...], cohesion[...]
    )
    inverse = state[15]
    rows = [x[k] + 0.5 * time_step * v[k] for k in range(3)]
    rows += [v[k] + 0.5 * time_step * acceleration[k] for k in range(3)]
    rows += [c * inverse for c in components]
    rows += [state[12], state[13], state[14], inverse]
    for k, row in enumerate(rows):
        state_out[k] = row
    gather_rims(rows, raw, lists, (s0, s1, s2, s3), blocks)


def end_kernel(
    lists, links, behind_depth, behind_strip, contact,
    acc_in, right, d_next, d_prev, s_next, s_prev, state, stress, plastic, cohesion, position, velocity,
    new_position, new_velocity, new_stress, new_plastic,
    acc, tmp, src, left, held, flag,
):
    cross_sums(
        lists, links, (behind_depth, behind_strip), (d_next, d_prev, s_next, s_prev),
        acc_in, right, acc, tmp, src, left, held,
    )
    _, half_v, acceleration, strain = rates_of(acc, state, contact, flag)
    components, hardened = plastic_return(
        elastic_step([stress[c] for c in range(6)], strain, 1.0), plastic[...], cohesion[...]
    )
    live = state[14]
    for k in range(3):
        new_position[k] = (position[k] + time_step * half_v[k]) * live
        new_velocity[k] = (velocity[k] + time_step * acceleration[k]) * live
    for c in range(6):
        new_stress[c] = components[c] * live
    new_plastic[...] = hardened * live


def shards(
    position, velocity, stress, plastic, particle_mass, density, cohesion,
    counts, block_pairs, pair_count, send_lists, cross_links, contact,
):
    position, velocity, stress = position[0, 0], velocity[0, 0], stress[0, 0]
    plastic, mass, density, cohesion = plastic[0, 0], particle_mass[0, 0], density[0, 0], cohesion[0, 0]
    counts, pairs, lists = counts[0, 0], block_pairs[0, 0], send_lists[0, 0]
    links, contact = cross_links[0, 0], contact[0, 0]
    blocks, parts = mass.shape
    rim = lists.shape[1]
    smem = pl.BlockSpec(memory_space=pltpu.SMEM)
    vmem = pl.BlockSpec(memory_space=pltpu.VMEM)
    shape = jax.ShapeDtypeStruct
    state_shape = shape((STATE, blocks, parts), f32)
    send_shape = shape((rim * STATE, parts), f32)
    acc_shape = shape((blocks, ROWS, parts), f32)
    right_shape = shape((blocks, FEATURES, parts), bf16)
    far_scratch = [
        pltpu.VMEM((blocks, ROWS, parts), f32),
        pltpu.VMEM((4 * rim * PITCH, parts), f32),
        pltpu.VMEM((4 * rim, 2 * ROWS, parts), bf16),
        pltpu.VMEM((4 * rim, parts, FEATURES), bf16),
        pltpu.VMEM((8, parts, parts), bf16),
        pltpu.VMEM((blocks + 8, parts), f32),
    ]
    raw_scratch = pltpu.VMEM((blocks * STATE, parts), f32)
    params = pltpu.CompilerParams(vmem_limit_bytes=24 << 20)

    behind_depth = from_behind(links[0], "depth", 1)
    behind_strip = passed_along(links[1], "strip", 1)

    def exchange(sends):
        return (
            from_behind(sends[1], "depth", -1),
            from_behind(sends[0], "depth", 1),
            passed_along(sends[3], "strip", -1),
            passed_along(sends[2], "strip", 1),
        )

    def local(state):
        tiles = pairs.shape[0]
        return pl.pallas_call(
            local_kernel,
            out_shape=(acc_shape, right_shape),
            in_specs=[smem, smem, vmem],
            out_specs=(vmem, vmem),
            scratch_shapes=[
                pltpu.VMEM((blocks * PITCH, parts), f32),
                pltpu.VMEM((blocks, 2 * ROWS, parts), bf16),
                pltpu.VMEM((blocks, parts, FEATURES), bf16),
                pltpu.VMEM((2 * UNROLL, parts, parts), bf16),
            ],
            compiler_params=params,
            cost_estimate=pl.CostEstimate(
                flops=tiles * parts * parts * 600, bytes_accessed=8 << 20, transcendentals=0
            ),
            name="local_tiles",
        )(pairs, pair_count, state)

    state, *sends = pl.pallas_call(
        begin_kernel,
        out_shape=(state_shape,) + (send_shape,) * 4,
        in_specs=[smem] * 2 + [pl.BlockSpec(memory_space=pl.ANY)] * 5,
        out_specs=(vmem,) * 5,
        scratch_shapes=[pltpu.VMEM((blocks, parts), f32), raw_scratch]
        + [pltpu.VMEM(a.shape, f32) for a in (position, velocity, stress, mass, density)]
        + [pltpu.SemaphoreType.DMA((5,))],
        compiler_params=params,
        name="begin",
    )(counts, lists, position, velocity, stress, mass, density)
    far = exchange(sends)
    acc, right = local(state)
    half, *sends = pl.pallas_call(
        half_kernel,
        out_shape=(state_shape,) + (send_shape,) * 4,
        in_specs=[smem] * 5 + [vmem] * 10,
        out_specs=(vmem,) * 5,
        scratch_shapes=far_scratch + [raw_scratch],
        compiler_params=params,
        name="half_step",
    )(
        lists, links, behind_depth, behind_strip, contact,
        acc, right, *far, state, stress, plastic, cohesion,
    )
    far = exchange(sends)
    acc, right = local(half)
    outs = pl.pallas_call(
        end_kernel,
        out_shape=(
            shape(position.shape, f32),
            shape(velocity.shape, f32),
            shape(stress.shape, f32),
            shape(plastic.shape, f32),
        ),
        in_specs=[smem] * 5 + [vmem] * 12,
        out_specs=(vmem,) * 4,
        scratch_shapes=far_scratch,
        compiler_params=params,
        name="full_step",
    )(
        lists, links, behind_depth, behind_strip, contact,
        acc, right, *far, half, stress, plastic, cohesion, position, velocity,
    )
    return tuple(out[None, None] for out in outs)


def solution(mesh):
    def spec(rank):
        return P("strip", "depth", *([None] * (rank - 2)))

    return jax.shard_map(
        shards,
        mesh=mesh,
        in_specs=tuple(spec(r) for r in (5, 5, 5, 4, 4, 4, 4, 3, 4, 2, 4, 5, 3)),
        out_specs=tuple(spec(r) for r in (5, 5, 5, 4)),
        check_vma=False,
    )
```

```python
import functools

import jax
import jax.numpy as jnp
from jax import lax
from jax.experimental import pallas as pl
from jax.experimental.pallas import tpu as pltpu
from jax.sharding import PartitionSpec as P

RETURN_ITERS = 4

smooth_len = 1.5
kernel_coef = -105.0 / (3.141592653589793 * 1.5**5)
time_step = 0.25
gravity = 1.0
spin_rate = 2.0
blade_stiff = 4.0
bulk_mod = 2.0
shear_mod = 1.5
friction = 0.25
harden_scale = 0.05
harden_mod = 0.5
relax_rate = 0.7
tau_floor = 0.5
voigt_index = ((0, 3, 5), (3, 1, 4), (5, 4, 2))
voigt_pairs = ((0, 0), (1, 1), (2, 2), (0, 1), (1, 2), (0, 2))

STATE = 16
SOURCES = 26
ROWS = 32
FEATURES = 32
UNROLL = 4
PITCH = 36
f32 = jnp.float32
bf16 = jnp.bfloat16


def from_behind(block, axis, distance):
    devices = range(lax.axis_size(axis))
    route = [(i - distance, i) for i in devices if i - distance in devices]
    return lax.ppermute(block, axis, route)


def passed_along(value, axis, steps):
    count = lax.axis_size(axis)
    pairs = [(source, (source + steps) % count) for source in range(count)]
    return lax.ppermute(value, axis, pairs)


def source_rows(x, v, s, mass, volume):
    rows = [mass]
    rows += [mass * x[k] for k in range(3)]
    rows += [mass * s[c] for c in range(6)]
    for k in range(3):
        i = voigt_index[k]
        rows.append(mass * (s[i[0]] * x[0] + s[i[1]] * x[1] + s[i[2]] * x[2]))
    rows.append(volume)
    rows += [volume * v[k] for k in range(3)]
    rows += [volume * x[k] for k in range(3)]
    for a, b in voigt_pairs:
        rows.append(volume * (0.5 * (v[a] * x[b] + v[b] * x[a])))
    return rows


def split3(value):
    high = value.astype(bf16).astype(f32)
    rest = value - high
    mid = rest.astype(bf16).astype(f32)
    low = (rest - mid).astype(bf16).astype(f32)
    return high, mid, low


PRODUCTS = ((0, 0), (0, 1), (1, 0), (1, 1), (0, 2), (2, 0))


def distance_rows(x, row_side, col_side):
    scaled = [x[k] * (1.0 / smooth_len) for k in range(3)]
    parts = [split3(y) for y in scaled]
    norm = split3(scaled[0] * scaled[0] + scaled[1] * scaled[1] + scaled[2] * scaled[2])
    one = jnp.ones_like(x[0])
    zero = jnp.zeros_like(x[0])
    left, right = [], []
    for k in range(3):
        for a, b in PRODUCTS:
            left.append(-2.0 * parts[k][a])
            right.append(parts[k][b])
    left += list(norm) + [one] * 3
    right += [one] * 3 + list(norm)
    fill = FEATURES - len(left)
    return (left + [zero] * fill if row_side else None, right + [zero] * fill if col_side else None)


def put_rows(ref, rows, start, count, stride):
    for k, row in enumerate(rows):
        ref[pl.ds(start * stride + k, count, stride=stride), :] = row


def get_row(ref, k, count, stride):
    return ref[pl.ds(k, count, stride=stride), :]


def close_kernel(left, right, weight):
    squared = lax.dot_general(left, right, (((1,), (0,)), ((), ())), preferred_element_type=f32)
    squared = jnp.maximum(squared, 1e-30)
    near = jnp.maximum(1.0 - squared * lax.rsqrt(squared), 0.0)
    cubed = near * near * (near if weight is None else near * weight)
    return cubed.astype(bf16)


def fold(result):
    return result[:ROWS] + result[ROWS:]


def to_rows(sources, kernel):
    return fold(
        lax.dot_general(sources, kernel, (((1,), (1,)), ((), ())), preferred_element_type=f32)
    )


def to_cols(sources, kernel):
    return fold(
        lax.dot_general(sources, kernel, (((1,), (0,)), ((), ())), preferred_element_type=f32)
    )


def pipelined(groups, width, prepare, apply, acc):
    for u in range(width):
        prepare(0, u, 0)

    def step(i, carry):
        for half in range(2):
            g = 2 * i + half
            found = []
            for u in range(width):
                found += apply(g, u, half)
                prepare(g + 1, u, 1 - half)
            for at, value in found:
                acc[at] += value
        return carry

    lax.fori_loop(0, (groups + 1) // 2, step, 0)


def store_sources(tmp, src, start, count):
    def one(b, carry):
        rows = tmp[pl.ds(b * PITCH, ROWS), :]
        high = rows.astype(bf16)
        src[start + b, 0:ROWS, :] = high
        src[start + b, ROWS : 2 * ROWS, :] = (rows - high.astype(f32)).astype(bf16)
        return carry

    lax.fori_loop(0, count, one, 0, unroll=4)


def store_cols(tmp, col, start, count):
    def one(b, carry):
        col[start + b] = tmp[pl.ds(b * PITCH, FEATURES), :].astype(bf16)
        return carry

    lax.fori_loop(0, count, one, 0, unroll=4)


def store_lefts(tmp, left, start, count):
    def one(b, carry):
        left[start + b] = tmp[pl.ds(b * PITCH, FEATURES), :].T.astype(bf16)
        return carry

    lax.fori_loop(0, count, one, 0, unroll=4)


def gather_rims(rows, raw, lists, sends, blocks):
    put_rows(raw, rows, 0, blocks, STATE)
    for face in range(4):
        for slot in range(lists.shape[1]):
            at = pl.multiple_of(lists[face, slot] * STATE, STATE)
            sends[face][slot * STATE : (slot + 1) * STATE, :] = raw[pl.ds(at, STATE), :]


def begin_kernel(
    counts, lists, links, pos_in, vel_in, stress_in, mass_in, density_in, state, s0, s1, s2, s3,
    occ, raw, pos, vel, stress, mass, density, sems,
):
    moved = ((pos_in, pos), (vel_in, vel), (stress_in, stress), (mass_in, mass), (density_in, density))
    copies = [pltpu.make_async_copy(a, b, sems.at[i]) for i, (a, b) in enumerate(moved)]
    for copy in copies:
        copy.start()
    blocks, parts = mass.shape
    lane = lax.broadcasted_iota(jnp.int32, (1, parts), 1)
    for b in range(blocks):
        occ[b : b + 1, :] = jnp.where(lane < counts[b], 1.0, 0.0)
    live = occ[...]
    for copy in copies:
        copy.wait()
    rho = density[...]
    inverse = 1.0 / (rho * rho)
    weighted = mass[...] * live * kernel_coef
    rows = [pos[k] for k in range(3)] + [vel[k] for k in range(3)]
    rows += [stress[c] * inverse for c in range(6)]
    rows += [weighted, weighted / rho, live, inverse]
    for k, row in enumerate(rows):
        state[k] = row
    gather_rims(rows, raw, lists, (s0, s1, s2, s3), blocks)
    cross = links.shape[1]
    for face, send in ((0, s0), (1, s2)):
        packed = jnp.zeros((1, parts), jnp.int32)
        for side in range(2):
            for q in range(cross):
                packed = jnp.where(lane == side * cross + q, links[face, q, side], packed)
        send[STATE - 1 : STATE, :] = packed.astype(f32)


def local_kernel(pairs, total, state, acc, right, tmp, src, left, held):
    blocks = state.shape[1]
    x = [state[k] for k in range(3)]
    v = [state[k] for k in range(3, 6)]
    s = [state[k] for k in range(6, 12)]
    zero = jnp.zeros_like(x[0])
    rows = source_rows(x, v, s, state[12], state[13])
    put_rows(tmp, rows + [zero] * (ROWS - SOURCES), 0, blocks, PITCH)
    store_sources(tmp, src, 0, blocks)
    left_rows, right_rows = distance_rows(x, True, True)
    put_rows(tmp, right_rows, 0, blocks, PITCH)
    store_cols(tmp, right, 0, blocks)
    put_rows(tmp, left_rows, 0, blocks, PITCH)

    store_lefts(tmp, left, 0, blocks)
    acc[...] = jnp.zeros(acc.shape, f32)
    live = total[0, 0]
    last = pairs.shape[0] - 1

    def entry(q):
        at = jnp.minimum(q, last)
        a, b = pairs[at, 0], pairs[at, 1]
        return jnp.where(q < live, a, 0), jnp.where(q < live, b, 0)

    def prepare(g, u, slot):
        q = g * UNROLL + u
        a, b = entry(q)
        weight = jnp.where(q < live, jnp.where(a == b, 0.5, 1.0), 0.0)
        held[slot * UNROLL + u] = close_kernel(left[a], right[b], weight)

    def apply(g, u, slot):
        a, b = entry(g * UNROLL + u)
        kernel = held[slot * UNROLL + u]
        return [(a, to_rows(src[b], kernel)), (b, to_cols(src[a], kernel))]

    pipelined((live + UNROLL - 1) // UNROLL, UNROLL, prepare, apply, acc)


def cross_sums(lists, links, links_behind, far, acc_in, right, acc, tmp, src, left, held):
    rim = lists.shape[1]
    for f in range(4):
        got = [get_row(far[f], k, rim, STATE) for k in range(14)]
        zero = jnp.zeros_like(got[0])
        rows = source_rows(got[0:3], got[3:6], got[6:12], got[12], got[13])
        put_rows(tmp, rows + [zero] * (ROWS - SOURCES), f * rim, rim, PITCH)
    store_sources(tmp, src, 0, 4 * rim)
    for f in range(4):
        got = [get_row(far[f], k, rim, STATE) for k in range(3)]
        put_rows(tmp, distance_rows(got, True, False)[0], f * rim, rim, PITCH)
    store_lefts(tmp, left, 0, 4 * rim)
    acc[...] = acc_in[...]

    last = links.shape[1] - 1

    def entry(q, u):
        at = jnp.minimum(q, last)
        face, behind = u // 2, u % 2
        if behind:
            own = lists[2 * face + 1, links_behind[face][1, at]]
            return own, u * rim + links_behind[face][0, at]
        return lists[2 * face, links[face, at, 0]], u * rim + links[face, at, 1]

    def prepare(q, u, slot):
        own, far_slot = entry(q, u)
        weight = None if links.shape[1] % 2 == 0 else jnp.where(q <= last, 1.0, 0.0)
        held[slot * 4 + u] = close_kernel(left[far_slot], right[own], weight)

    def apply(q, u, slot):
        own, far_slot = entry(q, u)
        return [(own, to_cols(src[far_slot], held[slot * 4 + u]))]

    pipelined(links.shape[1], 4, prepare, apply, acc)


def section_rates(summed, x, v, s, contact_flag):
    blade = (spin_rate * x[2], jnp.zeros_like(x[1]), -spin_rate * x[0])
    acceleration = []
    arm = [x[l] * summed[0] - summed[1 + l] for l in range(3)]
    for k in range(3):
        total = -summed[10 + k] + blade_stiff * contact_flag * (blade[k] - v[k])
        for l in range(3):
            slot = voigt_index[k][l]
            total = total + s[slot] * arm[l] + x[l] * summed[4 + slot]
        if k == 2:
            total = total - gravity
        acceleration.append(total)
    strain = []
    for c, (k, l) in enumerate(voigt_pairs):
        rate = 0.5 * (x[l] * summed[14 + k] + x[k] * summed[14 + l]) - summed[20 + c]
        rate = rate - 0.5 * summed[13] * (v[k] * x[l] + v[l] * x[k])
        rate = rate + 0.5 * (v[k] * summed[17 + l] + v[l] * summed[17 + k])
        strain.append(rate)
    return acceleration, strain


def elastic_step(stress, strain, fraction):
    volumetric = strain[0] + strain[1] + strain[2]
    lame_first = bulk_mod - 2.0 * shear_mod / 3.0
    components = []
    for c in range(6):
        change = 2.0 * shear_mod * strain[c]
        if c < 3:
            change = change + lame_first * volumetric
        components.append(stress[c] + fraction * time_step * change)
    return components


def plastic_return(c, plastic, cohesion):
    for _ in range(RETURN_ITERS):
        mean = (c[0] + c[1] + c[2]) / 3.0
        d = [c[0] - mean, c[1] - mean, c[2] - mean, c[3], c[4], c[5]]
        second = 0.5 * (d[0] * d[0] + d[1] * d[1] + d[2] * d[2])
        second = second + d[3] * d[3] + d[4] * d[4] + d[5] * d[5]
        tau = jnp.sqrt(second)
        limit = cohesion * (1.0 + plastic / (plastic + harden_scale))
        excess = jnp.maximum(tau + friction * 3.0 * mean - limit, 0.0)
        multiplier = (
            relax_rate * excess / (shear_mod + 9.0 * bulk_mod * friction * friction + harden_mod)
        )
        shrink = jnp.maximum(1.0 - shear_mod * multiplier / jnp.maximum(tau, tau_floor), 0.0)
        mean = mean - 3.0 * bulk_mod * friction * multiplier
        c = [
            d[0] * shrink + mean,
            d[1] * shrink + mean,
            d[2] * shrink + mean,
            d[3] * shrink,
            d[4] * shrink,
            d[5] * shrink,
        ]
        plastic = plastic + multiplier
    return c, plastic


def contact_rows(contact, flag, blocks):
    flag[...] = jnp.zeros_like(flag)
    for i in range(contact.shape[0]):
        flag[pl.ds(contact[i], 1), :] += 1.0
    return flag[0:blocks, :]


def rates_of(acc, state, contact, flag):
    blocks, parts = state.shape[1:]
    contact_flag = contact_rows(contact, flag, blocks)
    x = [state[k] for k in range(3)]
    v = [state[k] for k in range(3, 6)]
    s = [state[k] for k in range(6, 12)]
    summed = [acc[:, k, :] for k in range(SOURCES)]
    return x, v, *section_rates(summed, x, v, s, contact_flag)


def half_kernel(
    lists, links, behind_depth, behind_strip, contact,
    acc_in, right, d_next, d_prev, s_next, s_prev, state, stress, plastic, cohesion,
    state_out, s0, s1, s2, s3,
    acc, tmp, src, left, held, flag, raw,
):
    blocks = state.shape[1]
    cross_sums(
        lists, links, (behind_depth, behind_strip), (d_next, d_prev, s_next, s_prev),
        acc_in, right, acc, tmp, src, left, held,
    )
    x, v, acceleration, strain = rates_of(acc, state, contact, flag)
    components, _ = plastic_return(
        elastic_step([stress[c] for c in range(6)], strain, 0.5), plastic[...], cohesion[...]
    )
    inverse = state[15]
    rows = [x[k] + 0.5 * time_step * v[k] for k in range(3)]
    rows += [v[k] + 0.5 * time_step * acceleration[k] for k in range(3)]
    rows += [c * inverse for c in components]
    rows += [state[12], state[13], state[14], inverse]
    for k, row in enumerate(rows):
        state_out[k] = row
    gather_rims(rows, raw, lists, (s0, s1, s2, s3), blocks)


def end_kernel(
    lists, links, behind_depth, behind_strip, contact,
    acc_in, right, d_next, d_prev, s_next, s_prev, state, stress, plastic, cohesion, position, velocity,
    new_position, new_velocity, new_stress, new_plastic,
    acc, tmp, src, left, held, flag,
):
    cross_sums(
        lists, links, (behind_depth, behind_strip), (d_next, d_prev, s_next, s_prev),
        acc_in, right, acc, tmp, src, left, held,
    )
    _, half_v, acceleration, strain = rates_of(acc, state, contact, flag)
    components, hardened = plastic_return(
        elastic_step([stress[c] for c in range(6)], strain, 1.0), plastic[...], cohesion[...]
    )
    live = state[14]
    for k in range(3):
        new_position[k] = (position[k] + time_step * half_v[k]) * live
        new_velocity[k] = (velocity[k] + time_step * acceleration[k]) * live
    for c in range(6):
        new_stress[c] = components[c] * live
    new_plastic[...] = hardened * live


def shards(
    position, velocity, stress, plastic, particle_mass, density, cohesion,
    counts, block_pairs, pair_count, send_lists, cross_links, contact,
):
    position, velocity, stress = position[0, 0], velocity[0, 0], stress[0, 0]
    plastic, mass, density, cohesion = plastic[0, 0], particle_mass[0, 0], density[0, 0], cohesion[0, 0]
    counts, pairs, lists = counts[0, 0], block_pairs[0, 0], send_lists[0, 0]
    links, contact = cross_links[0, 0], contact[0, 0]
    blocks, parts = mass.shape
    rim = lists.shape[1]
    smem = pl.BlockSpec(memory_space=pltpu.SMEM)
    vmem = pl.BlockSpec(memory_space=pltpu.VMEM)
    shape = jax.ShapeDtypeStruct
    state_shape = shape((STATE, blocks, parts), f32)
    send_shape = shape((rim * STATE, parts), f32)
    acc_shape = shape((blocks, ROWS, parts), f32)
    right_shape = shape((blocks, FEATURES, parts), bf16)
    far_scratch = [
        pltpu.VMEM((blocks, ROWS, parts), f32),
        pltpu.VMEM((4 * rim * PITCH, parts), f32),
        pltpu.VMEM((4 * rim, 2 * ROWS, parts), bf16),
        pltpu.VMEM((4 * rim, parts, FEATURES), bf16),
        pltpu.VMEM((8, parts, parts), bf16),
        pltpu.VMEM((blocks + 8, parts), f32),
    ]
    raw_scratch = pltpu.VMEM((blocks * STATE, parts), f32)
    params = pltpu.CompilerParams(vmem_limit_bytes=24 << 20)

    cross = links.shape[1]

    def pair_list(rims):
        row = lax.slice(rims, (STATE - 1, 0), (STATE, 2 * cross))
        return row.reshape(2, cross).astype(jnp.int32)

    def exchange(sends):
        return (
            from_behind(sends[1], "depth", -1),
            from_behind(sends[0], "depth", 1),
            passed_along(sends[3], "strip", -1),
            passed_along(sends[2], "strip", 1),
        )

    def local(state):
        tiles = pairs.shape[0]
        return pl.pallas_call(
            local_kernel,
            out_shape=(acc_shape, right_shape),
            in_specs=[smem, smem, vmem],
            out_specs=(vmem, vmem),
            scratch_shapes=[
                pltpu.VMEM((blocks * PITCH, parts), f32),
                pltpu.VMEM((blocks, 2 * ROWS, parts), bf16),
                pltpu.VMEM((blocks, parts, FEATURES), bf16),
                pltpu.VMEM((2 * UNROLL, parts, parts), bf16),
            ],
            compiler_params=params,
            cost_estimate=pl.CostEstimate(
                flops=tiles * parts * parts * 600, bytes_accessed=8 << 20, transcendentals=0
            ),
            name="local_tiles",
        )(pairs, pair_count, state)

    state, *sends = pl.pallas_call(
        begin_kernel,
        out_shape=(state_shape,) + (send_shape,) * 4,
        in_specs=[smem] * 3 + [pl.BlockSpec(memory_space=pltpu.MemorySpace.HBM)] * 5,
        out_specs=(vmem,) * 5,
        scratch_shapes=[pltpu.VMEM((blocks, parts), f32), raw_scratch]
        + [pltpu.VMEM(a.shape, f32) for a in (position, velocity, stress, mass, density)]
        + [pltpu.SemaphoreType.DMA((5,))],
        compiler_params=params,
        name="begin",
    )(counts, lists, links, position, velocity, stress, mass, density)
    far = exchange(sends)
    behind_depth, behind_strip = pair_list(far[1]), pair_list(far[3])
    acc, right = local(state)
    half, *sends = pl.pallas_call(
        half_kernel,
        out_shape=(state_shape,) + (send_shape,) * 4,
        in_specs=[smem] * 5 + [vmem] * 10,
        out_specs=(vmem,) * 5,
        scratch_shapes=far_scratch + [raw_scratch],
        compiler_params=params,
        name="half_step",
    )(
        lists, links, behind_depth, behind_strip, contact,
        acc, right, *far, state, stress, plastic, cohesion,
    )
    far = exchange(sends)
    acc, right = local(half)
    outs = pl.pallas_call(
        end_kernel,
        out_shape=(
            shape(position.shape, f32),
            shape(velocity.shape, f32),
            shape(stress.shape, f32),
            shape(plastic.shape, f32),
        ),
        in_specs=[smem] * 5 + [vmem] * 12,
        out_specs=(vmem,) * 4,
        scratch_shapes=far_scratch,
        compiler_params=params,
        name="full_step",
    )(
        lists, links, behind_depth, behind_strip, contact,
        acc, right, *far, half, stress, plastic, cohesion, position, velocity,
    )
    return tuple(out[None, None] for out in outs)


def solution(mesh):
    def spec(rank):
        return P("strip", "depth", *([None] * (rank - 2)))

    return jax.shard_map(
        shards,
        mesh=mesh,
        in_specs=tuple(spec(r) for r in (5, 5, 5, 4, 4, 4, 4, 3, 4, 2, 4, 5, 3)),
        out_specs=tuple(spec(r) for r in (5, 5, 5, 4)),
        check_vma=False,
    )
```
